32 devices in a mesh: gx: 4 (over z), gy: 4 (over x, core), gz: 2 (over y).
Axes of the slice: x: 2, y: 2, z: 4, core: 2. Of those that a mesh axis runs over, the one named last changes fastest.
Arguments:
- right_sides: float32 [2, 32, 1024, 1024], P(None, ('gx', 'gy', 'gz')), may hold values from -6 to 6
- projector: float32 [2, 32, 1024, 192], P(None, ('gx', 'gy', 'gz')), may hold values from -0.1875 to 0.1875
- mixing: float32 [6, 2, 32, 2, 192, 192], P(None, None, ('gx', 'gy', 'gz')), may hold values from -0.3125 to 0.3125
- expander: float32 [64, 1024, 192], P(('gx', 'gy', 'gz')), may hold values from -0.4375 to 0.4375
Outputs:
- product: float32 [64, 1024, 1024], P(('gx', 'gy', 'gz'))
The draws below stay inside these ranges and needn't reach their ends.
All inputs are finite; a program needn't handle non-finite values.
Results may differ from the reference program's by a relative error of at most 0.0001.
Values sent between devices are 32-bit elements; how exact they have to be, the bound alone decides.
A program may use at most 128 MiB of HBM per device.

```python
import jax
import jax.numpy as jnp
from jax import lax

LEAF = 1024
K = 192
RHS = 1024
NODES = 64
LEVELS = 6
DEVICES = 32


def levels(key, dims, pieces, smallest, top_value):
    gain = 1.0
    for position, blocks in pieces:
        draws = jax.random.uniform(jax.random.fold_in(jax.random.fold_in(key, 6), position), (blocks,), jnp.float32, smallest / len(pieces), top_value / len(pieces))
        gain = gain * jnp.repeat(jnp.exp(draws), dims[position] // blocks).reshape((-1,) + (1,) * (len(dims) - 1 - position))
    return gain


def scatter_about(key, extent, spread, limit, split=(), held_as=jnp.bfloat16):
    array = spread * jax.random.normal(key, extent, jnp.float32)
    if split:
        array = array * levels(key, extent, split, -0.22, 0.18)
    return jnp.clip(array, -limit, limit).astype(held_as)


def setup_inputs(seed: int = 0) -> dict:
    splits = jax.random.split(jax.random.key(seed), 5)
    return {
        "right_sides": scatter_about(splits[0], (2, DEVICES, LEAF, RHS), 1.0, 6.0, ((1, 32),), jnp.float32),
        "projector": scatter_about(splits[1], (2, DEVICES, LEAF, K), LEAF ** -0.5, 0.1875, ((1, 32),), jnp.float32),
        "mixing": scatter_about(splits[2], (LEVELS, 2, DEVICES, 2, K, K), (2 * K) ** -0.5, 0.3125, ((2, 32),), jnp.float32),
        "expander": scatter_about(splits[3], (NODES, LEAF, K), K ** -0.5, 0.4375, ((0, 32),), jnp.float32),
    }


exact = lax.Precision.HIGHEST


def mix_level(weights, coeffs, partner):
    local_term = jnp.einsum("nkj,njr->nkr", weights[:, 0], coeffs, precision=exact)
    remote_term = jnp.einsum("nkj,njr->nkr", weights[:, 1], partner, precision=exact)
    return local_term + remote_term


def reference(right_sides, projector, mixing, expander):
    leaf_data = right_sides.reshape(NODES, LEAF, RHS)
    leaf_proj = projector.reshape(NODES, LEAF, K)
    leaf_mix = mixing.reshape(LEVELS, NODES, 2, K, K)
    coeffs = jnp.einsum("nlk,nlr->nkr", leaf_proj, leaf_data, precision=exact)
    for level_index in range(LEVELS):
        stride = 2 ** level_index
        paired = coeffs.reshape(NODES // (2 * stride), 2, stride, K, RHS)
        partner = paired[:, ::-1].reshape(NODES, K, RHS)
        coeffs = mix_level(leaf_mix[level_index], coeffs, partner)
    bit_view = coeffs.reshape((2,) * LEVELS + (K, RHS))
    axis_order = tuple(range(LEVELS - 1, -1, -1)) + (LEVELS, LEVELS + 1)
    reordered = bit_view.transpose(axis_order).reshape(NODES, K, RHS)
    return jnp.einsum("nlk,nkr->nlr", expander, reordered, precision=exact)
```

```python
import functools

import jax
import jax.numpy as jnp
from jax import lax
from jax.experimental import pallas as pl
from jax.experimental.pallas import tpu as pltpu
from jax.sharding import PartitionSpec as P

AXES = ("gx", "gy", "gz")
CHUNKS = 8
BLOCKS = 4
ORDER = (
    15, 0, 10, 0, 13, 0, 12, 11, 21, 1, 2, 1, 14, 1, 2, 0, 0, 3, 0, 3, 4, 20, 2, 1, 2, 1, 3, 5, 2, 0, 4, 1, 3, 6, 5, 4,
    5, 3, 2, 1, 0, 4, 6, 2, 4, 6, 5, 5, 3, 7, 1, 6, 2, 7, 3, 4, 6, 5, 7, 4, 3, 8, 6, 5, 7, 8, 4, 6, 5, 7, 7, 6, 8, 8,
    7, 8, 8, 7, 8, 8,
)


def split(x):
    hi = x.astype(jnp.bfloat16)
    lo = (x - hi.astype(jnp.float32)).astype(jnp.bfloat16)
    return hi, lo


def product(a, b):
    dot = functools.partial(jnp.dot, preferred_element_type=jnp.float32)
    return dot(a[0], b[0]) + (dot(a[0], b[1]) + dot(a[1], b[0]))


def expand_kernel(e_ref, c_ref, o_ref):
    o_ref[0] = product(split(e_ref[0]), split(c_ref[0]))


def expand(expander, coeffs):
    nodes, leaf, k = expander.shape
    rhs = coeffs.shape[2]
    width = rhs // BLOCKS
    return pl.pallas_call(
        expand_kernel,
        grid=(nodes, BLOCKS),
        in_specs=[
            pl.BlockSpec((1, leaf, k), lambda n, c: (n, 0, 0)),
            pl.BlockSpec((1, k, width), lambda n, c: (n, 0, c)),
        ],
        out_specs=pl.BlockSpec((1, leaf, width), lambda n, c: (n, 0, c)),
        out_shape=jax.ShapeDtypeStruct((nodes, leaf, rhs), jnp.float32),
    )(expander, coeffs)


def plan(bits):
    slots, local = list(range(bits)), bits
    steps, places = [], {}

    def swap(slot, level):
        nonlocal local
        slots[slot], local = local, slots[slot]
        steps.append((slot, False, level))
        if level is not None:
            places[level] = (tuple(slots), local)

    def show(slot):
        steps.append((slot, True, slot))
        places[slot] = (tuple(slots), local)

    half = bits // 2
    show(0)
    for k in range(1, half):
        swap(k, k)
    if bits % 2:
        show(half)
    for k in reversed(range(1, half)):
        swap(bits - 1 - k, bits - 1 - k)
        swap(k, None)
    swap(0, None)
    ahead = (tuple(slots), local)
    swap(bits - 1, bits - 1)
    swap(0, bits)
    return steps, places, ahead


def order(bits, count, chunks):
    tasks = list(ORDER)
    whole = [tasks.count(s) == chunks for s in range(count + 1)] + [tasks.count(10 + i) for i in range(bits + 1)]
    if not all(whole) or len(tasks) != (count + 1) * chunks + bits + 3:
        timed = [(3 * c + 4 * s, s) for c in range(chunks) for s in range(count + 1)]
        timed += [(l - bits, 100 + l) for l in range(bits + 1)] + [(0, 200), (0, 201)]
        tasks = [task for _, task in sorted(timed)]
    else:
        tasks = [task if task < 10 else 90 + task if task < 20 else 180 + task for task in tasks]
    ticks, at = [[]], -count - 1
    for task in tasks:
        rank = task if task >= 100 else -task
        if rank <= at:
            ticks.append([])
        ticks[-1].append(task)
        at = rank
    return ticks


def butterfly_kernel(sizes, x_hbm, p_hbm, mix_hbm, o_ref, *scratch):
    bits = sum(size.bit_length() - 1 for size in sizes)
    levels = bits + 1
    steps, places, ahead = plan(bits)
    count = len(steps)
    values, arrived = scratch[:count], scratch[count : 2 * count]
    (
        xbuf, pbuf, p_hi, p_lo, mixes, packed, weights, early, relay, w_hi, w_lo,
        x_sem, p_sem, mix_sem, send, recv, w_send, w_recv,
    ) = scratch[2 * count :]
    chunks, _, k, width = values[0].shape
    part = k // 2
    coords = [lax.axis_index(name) for name in AXES]
    me = (coords[0] * sizes[1] + coords[1]) * sizes[2] + coords[2]

    def bit_of(device, b):
        return (device // (1 << b)) % 2

    def flip(device, b):
        return device + (1 - 2 * bit_of(device, b)) * (1 << b)

    def place(d):
        return {
            "gx": d // (sizes[1] * sizes[2]),
            "gy": (d // sizes[2]) % sizes[1],
            "gz": d % sizes[2],
        }

    mine = [bit_of(me, b) for b in range(bits)]

    def goes(layout, c):
        slots, local = layout
        of_node = mine + [c]
        return sum(of_node[slot] * (1 << b) for b, slot in enumerate(slots)), of_node[local]

    def comes(layout, index):
        slots, local = layout
        of_node = [None] * (bits + 1)
        for b, slot in enumerate(slots):
            of_node[slot] = mine[b]
        of_node[local] = index
        return sum(of_node[b] * (1 << b) for b in range(bits))

    def reverse(device):
        return sum(bit_of(device, b) * (1 << (bits - 1 - b)) for b in range(bits))

    def remote(src, dst, s_sem, r_sem, target):
        return pltpu.make_async_remote_copy(
            src_ref=src,
            dst_ref=dst,
            send_sem=s_sem,
            recv_sem=r_sem,
            device_id=place(target),
            device_id_type=pl.DeviceIdType.MESH,
        )

    def transfer(s, c):
        slot, full, _ = steps[s]
        src = values[s].at[c] if full else values[s].at[c, 1 - mine[slot]]
        return remote(src, arrived[s].at[c], send.at[s, c], recv.at[s, c], flip(me, slot))

    def straight(level, c):
        target, index = goes(ahead if level == bits - 1 else places[level], c)
        there = early if level == bits - 1 else weights.at[level]
        copy = remote(
            packed.at[level, c], there.at[index],
            w_send.at[level, c], w_recv.at[level, index], target,
        )
        return copy, target, index

    last = bits - 1
    hop = remote(
        early.at[1 - mine[last]], weights.at[last, mine[last]],
        w_send.at[bits + 1, 0], w_recv.at[bits + 1, 0], flip(me, last),
    )
    home = reverse(me)
    apart = mine[0] != mine[last]
    lower, upper = pl.ds(0, part), pl.ds(part, part)
    direct = remote(
        packed.at[bits, :, lower], weights.at[bits, :, lower],
        w_send.at[bits, 0], w_recv.at[bits, 0], home,
    )
    beside = remote(
        packed.at[bits, :, upper], weights.at[bits, :, upper],
        w_send.at[bits, 1], w_recv.at[bits, 1], home,
    )
    around = remote(
        packed.at[bits, :, upper], relay, w_send.at[bits, 1], w_recv.at[bits + 1, 1], flip(me, 0)
    )
    onward = remote(
        relay, weights.at[bits, :, upper],
        w_send.at[bits + 1, 1], w_recv.at[bits, 1], reverse(flip(me, 0)),
    )

    def when(condition, action):
        pl.when(condition)(action)

    def greet(target):
        pl.semaphore_signal(
            barrier, inc=1, device_id=place(target), device_id_type=pl.DeviceIdType.MESH
        )

    barrier = pltpu.get_barrier_semaphore()
    greeted = jnp.int32(bits)
    for b in range(bits):
        greet(flip(me, b))
    layouts = [places[level] for level in range(1, last)] + [ahead]
    for layout in layouts:
        for c in range(2):
            source = comes(layout, c)
            when(source != me, functools.partial(greet, source))
            greeted = greeted + (goes(layout, c)[0] != me).astype(jnp.int32)
    when(home != me, functools.partial(greet, home))
    greeted = greeted + (home != me).astype(jnp.int32)
    when(apart, functools.partial(greet, flip(home, 0)))
    greeted = greeted + jnp.logical_not(apart).astype(jnp.int32)

    def load_x(c):
        return pltpu.make_async_copy(
            x_hbm.at[:, :, pl.ds(pl.multiple_of(c * width, width), width)],
            xbuf.at[c % 2], x_sem.at[c % 2],
        )

    load_p = pltpu.make_async_copy(p_hbm, pbuf, p_sem)

    def load_mix(level):
        return pltpu.make_async_copy(mix_hbm.at[level], mixes.at[level], mix_sem.at[level])

    load_mix(0).start()
    load_p.start()
    load_x(0).start()
    load_x(1).start()
    for level in range(1, levels):
        load_mix(level).start()

    def send_weights(level):
        load_mix(level).wait()
        for c in range(2):
            packed[level, c] = jnp.concatenate([mixes[level, c, 0], mixes[level, c, 1]], axis=1)
        if level == 0:
            weights[0] = packed[0]
        elif level < bits:
            there = early if level == last else weights.at[level]
            for c in range(2):
                copy, target, index = straight(level, c)

                @pl.when(target != me)
                def _():
                    copy.start()

                @pl.when(target == me)
                def _():
                    there[index] = packed[level, c]
        else:

            @pl.when(home != me)
            def _():
                direct.start()

            @pl.when(home == me)
            def _():
                weights[bits] = packed[bits]

            @pl.when(apart)
            def _():
                around.start()

            @pl.when(jnp.logical_not(apart) & (home != me))
            def _():
                beside.start()

    def forward_last():
        for index in range(2):

            @pl.when(comes(ahead, index) != me)
            def _():
                remote(
                    packed.at[last, 0], early.at[index],
                    w_send.at[last, 0], w_recv.at[last, index], me,
                ).wait_recv()

        weights[last, mine[last]] = early[mine[last]]
        hop.start()

    def forward_relay():
        @pl.when(jnp.logical_not(apart))
        def _():
            around.wait_recv()
            onward.start()

    def take_weights(level):
        if level == 0:
            pass
        elif level < last:
            for index in range(2):

                @pl.when(comes(places[level], index) != me)
                def _():
                    remote(
                        packed.at[level, 0], weights.at[level, index],
                        w_send.at[level, 0], w_recv.at[level, index], me,
                    ).wait_recv()
        elif level == last:
            hop.wait_recv()
        else:

            @pl.when(home != me)
            def _():
                direct.wait_recv()
                beside.wait_recv()

        for index in range(2):
            w_hi[level, index], w_lo[level, index] = split(weights[level, index])

    def mixed(level, index, one, other):
        pair = [jnp.concatenate([a, b], axis=0) for a, b in zip(one, other)]
        return product((w_hi[level, index], w_lo[level, index]), pair)

    def task(s, c):
        if s == 0:
            load_x(c).wait()
            for n in range(2):
                values[0][c, n] = product((p_hi[n], p_lo[n]), split(xbuf[c % 2, n]))
            pl.when(c + 2 < chunks)(lambda: load_x(c + 2).start())
        else:
            slot, full, level = steps[s - 1]
            bit = mine[slot]
            columns = pl.ds(pl.multiple_of(c * width, width), width)
            out = o_ref.at[:, :, columns] if s == count else values[s].at[c]
            if level is not None:
                pl.when(c == 0)(lambda: take_weights(level))
            transfer(s - 1, c).wait_recv()
            own, other = values[s - 1].at[c], arrived[s - 1].at[c]
            if full:
                for n in range(2):
                    out[n] = mixed(level, n, split(own[n]), split(other[n]))
            elif level is None:
                out[bit] = own[bit]
                out[1 - bit] = other[...]
            else:
                a, b = split(own[bit]), split(other[...])
                out[bit] = mixed(level, bit, a, b)
                out[1 - bit] = mixed(level, 1 - bit, b, a)
        if s < count:
            transfer(s, c).start()

    timetable = order(bits, count, chunks)

    def due(t, task):
        words = [0] * (len(timetable) // 31 + 1)
        for i, tasks in enumerate(timetable):
            words[i // 31] |= (task in tasks) << (i % 31)
        word = jnp.int32(words[0])
        for i, other in enumerate(words[1:]):
            word = jnp.where(t >= 31 * (i + 1), other, word)
        return lax.shift_right_logical(word, t % 31) % 2

    def tick(t, carry):
        done = list(carry)
        for s in reversed(range(count + 1)):
            now = due(t, s)
            pl.when(now == 1)(functools.partial(task, s, done[s]))
            done[s] = done[s] + now
        for level in range(levels):
            pl.when(due(t, 100 + level) == 1)(functools.partial(send_weights, level))
        pl.when(due(t, 200) == 1)(forward_last)
        pl.when(due(t, 201) == 1)(forward_relay)
        return tuple(done)

    pl.semaphore_wait(barrier, greeted)
    load_p.wait()
    for n in range(2):
        p_hi[n], p_lo[n] = split(pbuf[n])
    lax.fori_loop(0, len(timetable), tick, (jnp.int32(0),) * (count + 1))

    def drain(c, carry):
        for s in range(count):
            transfer(s, c).wait_send()
        return carry

    lax.fori_loop(0, chunks, drain, 0)
    for level in range(1, bits):
        for c in range(2):
            copy, target, _ = straight(level, c)
            pl.when(target != me)(copy.wait_send)
    hop.wait_send()
    pl.when(home != me)(direct.wait_send)
    pl.when(apart)(around.wait_send)
    pl.when(jnp.logical_not(apart) & (home != me))(beside.wait_send)
    pl.when(jnp.logical_not(apart))(onward.wait_send)


def butterfly(sizes, data, proj, mix):
    _, leaf, rhs = data.shape
    k = proj.shape[1]
    levels = mix.shape[0]
    bits = levels - 1
    width = rhs // CHUNKS
    steps, _, _ = plan(bits)
    f32, bf16 = jnp.float32, jnp.bfloat16
    held = [pltpu.VMEM((CHUNKS, 2, k, width), f32) for _ in steps]
    landed = [pltpu.VMEM((CHUNKS,) + ((2,) if full else ()) + (k, width), f32) for _, full, _ in steps]
    dma = pltpu.SemaphoreType.DMA
    return pl.pallas_call(
        functools.partial(butterfly_kernel, sizes),
        out_shape=jax.ShapeDtypeStruct((2, k, rhs), f32),
        in_specs=[pl.BlockSpec(memory_space=pl.ANY)] * 3,
        out_specs=pl.BlockSpec(memory_space=pltpu.VMEM),
        scratch_shapes=held + landed + [
            pltpu.VMEM((2, 2, leaf, width), f32),
            pltpu.VMEM((2, k, leaf), f32),
            pltpu.VMEM((2, k, leaf), bf16),
            pltpu.VMEM((2, k, leaf), bf16),
            pltpu.VMEM((levels, 2, 2, k, k), f32),
            pltpu.VMEM((levels, 2, k, 2 * k), f32),
            pltpu.VMEM((levels, 2, k, 2 * k), f32),
            pltpu.VMEM((2, k, 2 * k), f32),
            pltpu.VMEM((2, k // 2, 2 * k), f32),
            pltpu.VMEM((levels, 2, k, 2 * k), bf16),
            pltpu.VMEM((levels, 2, k, 2 * k), bf16),
            dma((2,)),
            dma,
            dma((levels,)),
            dma((len(steps), CHUNKS)),
            dma((len(steps), CHUNKS)),
            dma((levels + 1, 2)),
            dma((levels + 1, 2)),
        ],
        compiler_params=pltpu.CompilerParams(
            collective_id=0, has_side_effects=True, vmem_limit_bytes=60 * 2**20
        ),
    )(data, proj, mix)


def shards(right_sides, projector, mixing, expander):
    sizes = tuple(lax.axis_size(name) for name in AXES)
    proj = jnp.swapaxes(projector[:, 0], 1, 2)
    return expand(expander, butterfly(sizes, right_sides[:, 0], proj, mixing[:, :, 0]))


def solution(mesh):
    placed = (
        P(None, AXES, None, None),
        P(None, AXES, None, None),
        P(None, None, AXES, None, None, None),
        P(AXES, None, None),
    )
    return jax.shard_map(
        shards, mesh=mesh, in_specs=placed, out_specs=P(AXES, None, None), check_vma=False
    )
```

```python
import functools

import jax
import jax.numpy as jnp
from jax import lax
from jax.experimental import pallas as pl
from jax.experimental.pallas import tpu as pltpu
from jax.sharding import PartitionSpec as P

AXES = ("gx", "gy", "gz")
CHUNKS = 8
ORDER = (
    15, 0, 10, 0, 13, 0, 12, 11, 21, 1, 2, 1, 14, 1, 2, 0, 0, 3, 0, 3, 4, 20, 2, 1, 2, 1, 3, 5, 2, 0, 4, 1, 3, 6, 5, 4,
    5, 3, 2, 1, 0, 4, 6, 2, 4, 6, 5, 5, 3, 7, 1, 6, 2, 7, 3, 4, 6, 5, 7, 4, 3, 8, 6, 5, 7, 8, 4, 6, 5, 7, 7, 6, 8, 8,
    7, 8, 8, 7, 8, 8,
)


def split(x):
    hi = x.astype(jnp.bfloat16)
    lo = (x - hi.astype(jnp.float32)).astype(jnp.bfloat16)
    return hi, lo


def product(a, b, over=((1,), (0,))):
    def dot(x, y):
        return lax.dot_general(x, y, (over, ((), ())), preferred_element_type=jnp.float32)

    return dot(a[0], b[0]) + (dot(a[0], b[1]) + dot(a[1], b[0]))


def expand_kernel(e_ref, c_ref, o_ref):
    o_ref[0] = product(split(e_ref[0]), split(c_ref[0]), ((0,), (0,)))


def expand(expander, coeffs):
    nodes, k, leaf = expander.shape
    rhs = coeffs.shape[2]
    return pl.pallas_call(
        expand_kernel,
        grid=(nodes,),
        in_specs=[
            pl.BlockSpec((1, k, leaf), lambda n: (n, 0, 0)),
            pl.BlockSpec((1, k, rhs), lambda n: (n, 0, 0)),
        ],
        out_specs=pl.BlockSpec((1, leaf, rhs), lambda n: (n, 0, 0)),
        out_shape=jax.ShapeDtypeStruct((nodes, leaf, rhs), jnp.float32),
        compiler_params=pltpu.CompilerParams(vmem_limit_bytes=32 * 2**20),
    )(expander, coeffs)


def plan(bits):
    slots, local = list(range(bits)), bits
    steps, places = [], {}

    def swap(slot, level):
        nonlocal local
        slots[slot], local = local, slots[slot]
        steps.append((slot, False, level))
        if level is not None:
            places[level] = (tuple(slots), local)

    def show(slot):
        steps.append((slot, True, slot))
        places[slot] = (tuple(slots), local)

    half = bits // 2
    show(0)
    for k in range(1, half):
        swap(k, k)
    if bits % 2:
        show(half)
    for k in reversed(range(1, half)):
        swap(bits - 1 - k, bits - 1 - k)
        swap(k, None)
    swap(0, None)
    ahead = (tuple(slots), local)
    swap(bits - 1, bits - 1)
    swap(0, bits)
    return steps, places, ahead


def order(bits, count, chunks):
    tasks = list(ORDER)
    whole = [tasks.count(s) == chunks for s in range(count + 1)] + [tasks.count(10 + i) for i in range(bits + 1)]
    if not all(whole) or len(tasks) != (count + 1) * chunks + bits + 3:
        timed = [(3 * c + 4 * s, s) for c in range(chunks) for s in range(count + 1)]
        timed += [(l - bits, 100 + l) for l in range(bits + 1)] + [(0, 200), (0, 201)]
        tasks = [task for _, task in sorted(timed)]
    else:
        tasks = [task if task < 10 else 90 + task if task < 20 else 180 + task for task in tasks]
    ticks, at = [[]], -count - 1
    for task in tasks:
        rank = task if task >= 100 else -task
        if rank <= at:
            ticks.append([])
        ticks[-1].append(task)
        at = rank
    return ticks


def butterfly_kernel(sizes, x_hbm, p_hbm, mix_hbm, o_ref, *scratch):
    bits = sum(size.bit_length() - 1 for size in sizes)
    levels = bits + 1
    steps, places, ahead = plan(bits)
    count = len(steps)
    values, arrived = scratch[:count], scratch[count : 2 * count]
    (
        xbuf, pbuf, p_hi, p_lo, mixes, packed, weights, early, relay, w_hi, w_lo,
        x_sem, p_sem, mix_sem, send, recv, w_send, w_recv,
    ) = scratch[2 * count :]
    chunks, _, k, width = values[0].shape
    part = k // 2
    coords = [lax.axis_index(name) for name in AXES]
    me = (coords[0] * sizes[1] + coords[1]) * sizes[2] + coords[2]

    def bit_of(device, b):
        return (device // (1 << b)) % 2

    def flip(device, b):
        return device + (1 - 2 * bit_of(device, b)) * (1 << b)

    def place(d):
        return {
            "gx": d // (sizes[1] * sizes[2]),
            "gy": (d // sizes[2]) % sizes[1],
            "gz": d % sizes[2],
        }

    mine = [bit_of(me, b) for b in range(bits)]

    def goes(layout, c):
        slots, local = layout
        of_node = mine + [c]
        return sum(of_node[slot] * (1 << b) for b, slot in enumerate(slots)), of_node[local]

    def comes(layout, index):
        slots, local = layout
        of_node = [None] * (bits + 1)
        for b, slot in enumerate(slots):
            of_node[slot] = mine[b]
        of_node[local] = index
        return sum(of_node[b] * (1 << b) for b in range(bits))

    def reverse(device):
        return sum(bit_of(device, b) * (1 << (bits - 1 - b)) for b in range(bits))

    def remote(src, dst, s_sem, r_sem, target):
        return pltpu.make_async_remote_copy(
            src_ref=src,
            dst_ref=dst,
            send_sem=s_sem,
            recv_sem=r_sem,
            device_id=place(target),
            device_id_type=pl.DeviceIdType.MESH,
        )

    def transfer(s, c):
        slot, full, _ = steps[s]
        src = values[s].at[c] if full else values[s].at[c, 1 - mine[slot]]
        return remote(src, arrived[s].at[c], send.at[s, c], recv.at[s, c], flip(me, slot))

    def straight(level, c):
        target, index = goes(ahead if level == bits - 1 else places[level], c)
        there = early if level == bits - 1 else weights.at[level]
        copy = remote(
            packed.at[level, c], there.at[index],
            w_send.at[level, c], w_recv.at[level, index], target,
        )
        return copy, target, index

    last = bits - 1
    hop = remote(
        early.at[1 - mine[last]], weights.at[last, mine[last]],
        w_send.at[bits + 1, 0], w_recv.at[bits + 1, 0], flip(me, last),
    )
    home = reverse(me)
    apart = mine[0] != mine[last]
    lower, upper = pl.ds(0, part), pl.ds(part, part)
    direct = remote(
        packed.at[bits, :, lower], weights.at[bits, :, lower],
        w_send.at[bits, 0], w_recv.at[bits, 0], home,
    )
    beside = remote(
        packed.at[bits, :, upper], weights.at[bits, :, upper],
        w_send.at[bits, 1], w_recv.at[bits, 1], home,
    )
    around = remote(
        packed.at[bits, :, upper], relay, w_send.at[bits, 1], w_recv.at[bits + 1, 1], flip(me, 0)
    )
    onward = remote(
        relay, weights.at[bits, :, upper],
        w_send.at[bits + 1, 1], w_recv.at[bits, 1], reverse(flip(me, 0)),
    )

    def when(condition, action):
        pl.when(condition)(action)

    def greet(target):
        pl.semaphore_signal(
            barrier, inc=1, device_id=place(target), device_id_type=pl.DeviceIdType.MESH
        )

    barrier = pltpu.get_barrier_semaphore()
    greeted = jnp.int32(bits)
    for b in range(bits):
        greet(flip(me, b))
    layouts = [places[level] for level in range(1, last)] + [ahead]
    for layout in layouts:
        for c in range(2):
            source = comes(layout, c)
            when(source != me, functools.partial(greet, source))
            greeted = greeted + (goes(layout, c)[0] != me).astype(jnp.int32)
    when(home != me, functools.partial(greet, home))
    greeted = greeted + (home != me).astype(jnp.int32)
    when(apart, functools.partial(greet, flip(home, 0)))
    greeted = greeted + jnp.logical_not(apart).astype(jnp.int32)

    def load_x(c):
        return pltpu.make_async_copy(
            x_hbm.at[:, :, pl.ds(pl.multiple_of(c * width, width), width)],
            xbuf.at[c % 2], x_sem.at[c % 2],
        )

    load_p = pltpu.make_async_copy(p_hbm, pbuf, p_sem)

    def load_mix(level):
        return pltpu.make_async_copy(mix_hbm.at[level], mixes.at[level], mix_sem.at[level])

    load_mix(bits).start()
    load_p.start()
    load_x(0).start()
    for level in range(bits):
        load_mix(level).start()
    load_x(1).start()

    def send_weights(level):
        load_mix(level).wait()
        for c in range(2):
            packed[level, c] = jnp.concatenate([mixes[level, c, 0], mixes[level, c, 1]], axis=1)
        if level == 0:
            weights[0] = packed[0]
        elif level < bits:
            there = early if level == last else weights.at[level]
            for c in range(2):
                copy, target, index = straight(level, c)

                @pl.when(target != me)
                def _():
                    copy.start()

                @pl.when(target == me)
                def _():
                    there[index] = packed[level, c]
        else:

            @pl.when(home != me)
            def _():
                direct.start()

            @pl.when(home == me)
            def _():
                weights[bits] = packed[bits]

            @pl.when(apart)
            def _():
                around.start()

            @pl.when(jnp.logical_not(apart) & (home != me))
            def _():
                beside.start()

    def forward_last():
        for index in range(2):

            @pl.when(comes(ahead, index) != me)
            def _():
                remote(
                    packed.at[last, 0], early.at[index],
                    w_send.at[last, 0], w_recv.at[last, index], me,
                ).wait_recv()

        weights[last, mine[last]] = early[mine[last]]
        hop.start()

    def forward_relay():
        @pl.when(jnp.logical_not(apart))
        def _():
            around.wait_recv()
            onward.start()

    def take_weights(level):
        if level == 0:
            pass
        elif level < last:
            for index in range(2):

                @pl.when(comes(places[level], index) != me)
                def _():
                    remote(
                        packed.at[level, 0], weights.at[level, index],
                        w_send.at[level, 0], w_recv.at[level, index], me,
                    ).wait_recv()
        elif level == last:
            hop.wait_recv()
        else:

            @pl.when(home != me)
            def _():
                direct.wait_recv()
                beside.wait_recv()

        for index in range(2):
            w_hi[level, index], w_lo[level, index] = split(weights[level, index])

    def mixed(level, index, one, other):
        pair = [jnp.concatenate([a, b], axis=0) for a, b in zip(one, other)]
        return product((w_hi[level, index], w_lo[level, index]), pair)

    def task(s, c):
        if s == 0:

            @pl.when(c == 0)
            def _():
                load_p.wait()
                for n in range(2):
                    p_hi[n], p_lo[n] = split(pbuf[n])

            load_x(c).wait()
            for n in range(2):
                values[0][c, n] = product((p_hi[n], p_lo[n]), split(xbuf[c % 2, n]))
            pl.when(c + 2 < chunks)(lambda: load_x(c + 2).start())
        else:
            slot, full, level = steps[s - 1]
            bit = mine[slot]
            columns = pl.ds(pl.multiple_of(c * width, width), width)
            out = o_ref.at[:, :, columns] if s == count else values[s].at[c]
            if level is not None:
                pl.when(c == 0)(lambda: take_weights(level))
            transfer(s - 1, c).wait_recv()
            own, other = values[s - 1].at[c], arrived[s - 1].at[c]
            if full:
                for n in range(2):
                    out[n] = mixed(level, n, split(own[n]), split(other[n]))
            elif level is None:
                out[bit] = own[bit]
                out[1 - bit] = other[...]
            else:
                a, b = split(own[bit]), split(other[...])
                out[bit] = mixed(level, bit, a, b)
                out[1 - bit] = mixed(level, 1 - bit, b, a)
        if s < count:
            transfer(s, c).start()

    timetable = order(bits, count, chunks)

    def due(t, *kinds):
        words = [0] * (len(timetable) // 31 + 1)
        for i, tasks in enumerate(timetable):
            words[i // 31] |= any(kind in tasks for kind in kinds) << (i % 31)
        word = jnp.int32(words[0])
        for i, other in enumerate(words[1:]):
            word = jnp.where(t >= 31 * (i + 1), other, word)
        return lax.shift_right_logical(word, t % 31) % 2

    def tick(t, carry):
        done = list(carry)
        for s in reversed(range(count + 1)):
            now = due(t, s)
            pl.when(now == 1)(functools.partial(task, s, done[s]))
            done[s] = done[s] + now
        others = [(100 + level, functools.partial(send_weights, level)) for level in range(levels)]
        others += [(200, forward_last), (201, forward_relay)]

        @pl.when(due(t, *(kind for kind, _ in others)) == 1)
        def _():
            for kind, action in others:
                pl.when(due(t, kind) == 1)(action)

        return tuple(done)

    pl.semaphore_wait(barrier, greeted)
    lax.fori_loop(0, len(timetable), tick, (jnp.int32(0),) * (count + 1))

    def drain(c, carry):
        for s in range(count):
            transfer(s, c).wait_send()
        return carry

    lax.fori_loop(0, chunks, drain, 0)
    for level in range(1, bits):
        for c in range(2):
            copy, target, _ = straight(level, c)
            pl.when(target != me)(copy.wait_send)
    hop.wait_send()
    pl.when(home != me)(direct.wait_send)
    pl.when(apart)(around.wait_send)
    pl.when(jnp.logical_not(apart) & (home != me))(beside.wait_send)
    pl.when(jnp.logical_not(apart))(onward.wait_send)


def butterfly(sizes, data, proj, mix):
    _, leaf, rhs = data.shape
    k = proj.shape[1]
    levels = mix.shape[0]
    bits = levels - 1
    width = rhs // CHUNKS
    steps, _, _ = plan(bits)
    f32, bf16 = jnp.float32, jnp.bfloat16
    held = [pltpu.VMEM((CHUNKS, 2, k, width), f32) for _ in steps]
    landed = [pltpu.VMEM((CHUNKS,) + ((2,) if full else ()) + (k, width), f32) for _, full, _ in steps]
    dma = pltpu.SemaphoreType.DMA
    return pl.pallas_call(
        functools.partial(butterfly_kernel, sizes),
        out_shape=jax.ShapeDtypeStruct((2, k, rhs), f32),
        in_specs=[pl.BlockSpec(memory_space=pltpu.HBM)] * 3,
        out_specs=pl.BlockSpec(memory_space=pltpu.VMEM),
        scratch_shapes=held + landed + [
            pltpu.VMEM((2, 2, leaf, width), f32),
            pltpu.VMEM((2, k, leaf), f32),
            pltpu.VMEM((2, k, leaf), bf16),
            pltpu.VMEM((2, k, leaf), bf16),
            pltpu.VMEM((levels, 2, 2, k, k), f32),
            pltpu.VMEM((levels, 2, k, 2 * k), f32),
            pltpu.VMEM((levels, 2, k, 2 * k), f32),
            pltpu.VMEM((2, k, 2 * k), f32),
            pltpu.VMEM((2, k // 2, 2 * k), f32),
            pltpu.VMEM((levels, 2, k, 2 * k), bf16),
            pltpu.VMEM((levels, 2, k, 2 * k), bf16),
            dma((2,)),
            dma,
            dma((levels,)),
            dma((len(steps), CHUNKS)),
            dma((len(steps), CHUNKS)),
            dma((levels + 1, 2)),
            dma((levels + 1, 2)),
        ],
        compiler_params=pltpu.CompilerParams(
            collective_id=0, has_side_effects=True, vmem_limit_bytes=(46 + levels) * 2**20
        ),
    )(data, proj, mix)


def shards(right_sides, projector, mixing, expander):
    sizes = tuple(lax.axis_size(name) for name in AXES)
    proj = jnp.swapaxes(projector[:, 0], 1, 2)
    return expand(jnp.swapaxes(expander, 1, 2), butterfly(sizes, right_sides[:, 0], proj, mixing[:, :, 0]))


def solution(mesh):
    placed = (
        P(None, AXES, None, None),
        P(None, AXES, None, None),
        P(None, None, AXES, None, None, None),
        P(AXES, None, None),
    )
    return jax.shard_map(
        shards, mesh=mesh, in_specs=placed, out_specs=P(AXES, None, None), check_vma=False
    )
```

```python
import functools

import jax
import jax.numpy as jnp
from jax import lax
from jax.experimental import pallas as pl
from jax.experimental.pallas import tpu as pltpu
from jax.sharding import PartitionSpec as P

AXES = ("gx", "gy", "gz")
CHUNKS = 8
ORDER = (
    15, 13, 0, 0, 12, 21, 0, 14, 11, 10, 1, 0, 1, 2, 2, 1, 3, 2, 0, 0, 3, 20, 4, 3, 1, 2, 1, 5, 0, 4, 2, 1, 3, 5, 6, 4,
    2, 5, 4, 3, 1, 0, 6, 3, 6, 4, 5, 2, 1, 5, 4, 7, 7, 6, 2, 3, 5, 7, 6, 4, 3, 6, 5, 7, 4, 6, 5, 7, 8, 6, 8, 7,
    8, 7, 8, 8, 7, 8, 8, 8,
)


def split(x):
    hi = x.astype(jnp.bfloat16)
    lo = (x - hi.astype(jnp.float32)).astype(jnp.bfloat16)
    return hi, lo


def product(a, b, over=((1,), (0,))):
    def dot(x, y):
        return lax.dot_general(x, y, (over, ((), ())), preferred_element_type=jnp.float32)

    return dot(a[0], b[0]) + (dot(a[0], b[1]) + dot(a[1], b[0]))


def expand_kernel(e_ref, c_ref, o_ref):
    o_ref[0] = product(split(e_ref[0]), split(c_ref[0]), ((0,), (0,)))


def expand(expander, coeffs):
    nodes, k, leaf = expander.shape
    rhs = coeffs.shape[2]
    return pl.pallas_call(
        expand_kernel,
        grid=(nodes,),
        in_specs=[
            pl.BlockSpec((1, k, leaf), lambda n: (n, 0, 0)),
            pl.BlockSpec((1, k, rhs), lambda n: (n, 0, 0)),
        ],
        out_specs=pl.BlockSpec((1, leaf, rhs), lambda n: (n, 0, 0)),
        out_shape=jax.ShapeDtypeStruct((nodes, leaf, rhs), jnp.float32),
        compiler_params=pltpu.CompilerParams(vmem_limit_bytes=32 * 2**20),
    )(expander, coeffs)


def plan(bits):
    slots, local = list(range(bits)), bits
    steps, places = [], {}

    def swap(slot, level):
        nonlocal local
        slots[slot], local = local, slots[slot]
        steps.append((slot, False, level))
        if level is not None:
            places[level] = (tuple(slots), local)

    def show(slot):
        steps.append((slot, True, slot))
        places[slot] = (tuple(slots), local)

    half = bits // 2
    show(0)
    for k in range(1, half):
        swap(k, k)
    if bits % 2:
        show(half)
    for k in reversed(range(1, half)):
        swap(bits - 1 - k, bits - 1 - k)
        swap(k, None)
    swap(0, None)
    ahead = (tuple(slots), local)
    swap(bits - 1, bits - 1)
    swap(0, bits)
    return steps, places, ahead


def order(bits, count, chunks):
    tasks = list(ORDER)
    whole = [tasks.count(s) == chunks for s in range(count + 1)] + [tasks.count(10 + i) for i in range(bits + 1)]
    if not all(whole) or len(tasks) != (count + 1) * chunks + bits + 3:
        timed = [(3 * c + 4 * s, s) for c in range(chunks) for s in range(count + 1)]
        timed += [(l - bits, 100 + l) for l in range(bits + 1)] + [(0, 200), (0, 201)]
        tasks = [task for _, task in sorted(timed)]
    else:
        tasks = [task if task < 10 else 90 + task if task < 20 else 180 + task for task in tasks]
    ticks, at = [[]], -count - 1
    for task in tasks:
        rank = task if task >= 100 else -task
        if rank <= at:
            ticks.append([])
        ticks[-1].append(task)
        at = rank
    return ticks


def butterfly_kernel(sizes, x_hbm, p_hbm, mix_hbm, o_ref, *scratch):
    bits = sum(size.bit_length() - 1 for size in sizes)
    levels = bits + 1
    steps, places, ahead = plan(bits)
    count = len(steps)
    values, arrived = scratch[:count], scratch[count : 2 * count]
    (
        xbuf, pbuf, p_hi, p_lo, mixes, packed, weights, early, relay, w_hi, w_lo,
        x_sem, p_sem, mix_sem, send, recv, w_send, w_recv,
    ) = scratch[2 * count :]
    chunks, _, k, width = values[0].shape
    part = k // 2
    coords = [lax.axis_index(name) for name in AXES]
    me = (coords[0] * sizes[1] + coords[1]) * sizes[2] + coords[2]

    def bit_of(device, b):
        return (device // (1 << b)) % 2

    def flip(device, b):
        return device + (1 - 2 * bit_of(device, b)) * (1 << b)

    def place(d):
        return {
            "gx": d // (sizes[1] * sizes[2]),
            "gy": (d // sizes[2]) % sizes[1],
            "gz": d % sizes[2],
        }

    mine = [bit_of(me, b) for b in range(bits)]

    def goes(layout, c):
        slots, local = layout
        of_node = mine + [c]
        return sum(of_node[slot] * (1 << b) for b, slot in enumerate(slots)), of_node[local]

    def comes(layout, index):
        slots, local = layout
        of_node = [None] * (bits + 1)
        for b, slot in enumerate(slots):
            of_node[slot] = mine[b]
        of_node[local] = index
        return sum(of_node[b] * (1 << b) for b in range(bits))

    def reverse(device):
        return sum(bit_of(device, b) * (1 << (bits - 1 - b)) for b in range(bits))

    def remote(src, dst, s_sem, r_sem, target):
        return pltpu.make_async_remote_copy(
            src_ref=src,
            dst_ref=dst,
            send_sem=s_sem,
            recv_sem=r_sem,
            device_id=place(target),
            device_id_type=pl.DeviceIdType.MESH,
        )

    def transfer(s, c):
        slot, full, _ = steps[s]
        src = values[s].at[c] if full else values[s].at[c, 1 - mine[slot]]
        return remote(src, arrived[s].at[c], send.at[s, c], recv.at[s, c], flip(me, slot))

    def straight(level, c):
        target, index = goes(ahead if level == bits - 1 else places[level], c)
        there = early if level == bits - 1 else weights.at[level]
        copy = remote(
            packed.at[level, c], there.at[index],
            w_send.at[level, c], w_recv.at[level, index], target,
        )
        return copy, target, index

    last = bits - 1
    hop = remote(
        early.at[1 - mine[last]], weights.at[last, mine[last]],
        w_send.at[bits + 1, 0], w_recv.at[bits + 1, 0], flip(me, last),
    )
    home = reverse(me)
    apart = mine[0] != mine[last]
    lower, upper = pl.ds(0, part), pl.ds(part, part)
    direct = remote(
        packed.at[bits, :, lower], weights.at[bits, :, lower],
        w_send.at[bits, 0], w_recv.at[bits, 0], home,
    )
    beside = remote(
        packed.at[bits, :, upper], weights.at[bits, :, upper],
        w_send.at[bits, 1], w_recv.at[bits, 1], home,
    )
    around = remote(
        packed.at[bits, :, upper], relay, w_send.at[bits, 1], w_recv.at[bits + 1, 1], flip(me, 0)
    )
    onward = remote(
        relay, weights.at[bits, :, upper],
        w_send.at[bits + 1, 1], w_recv.at[bits, 1], reverse(flip(me, 0)),
    )

    def when(condition, action):
        pl.when(condition)(action)

    def greet(target):
        pl.semaphore_signal(
            barrier, inc=1, device_id=place(target), device_id_type=pl.DeviceIdType.MESH
        )

    barrier = pltpu.get_barrier_semaphore()
    greeted = jnp.int32(bits)
    for b in range(bits):
        greet(flip(me, b))
    layouts = [places[level] for level in range(1, last)] + [ahead]
    for layout in layouts:
        for c in range(2):
            source = comes(layout, c)
            when(source != me, functools.partial(greet, source))
            greeted = greeted + (goes(layout, c)[0] != me).astype(jnp.int32)
    when(home != me, functools.partial(greet, home))
    greeted = greeted + (home != me).astype(jnp.int32)
    when(apart, functools.partial(greet, flip(home, 0)))
    greeted = greeted + jnp.logical_not(apart).astype(jnp.int32)

    def load_x(c):
        return pltpu.make_async_copy(
            x_hbm.at[:, :, pl.ds(pl.multiple_of(c * width, width), width)],
            xbuf.at[c % 2], x_sem.at[c % 2],
        )

    load_p = pltpu.make_async_copy(p_hbm, pbuf, p_sem)

    def load_mix(level):
        return pltpu.make_async_copy(mix_hbm.at[level], mixes.at[level], mix_sem.at[level])

    load_mix(bits).start()
    load_p.start()
    load_x(0).start()
    for level in range(bits):
        load_mix(level).start()
    load_x(1).start()

    def send_weights(level):
        load_mix(level).wait()
        for c in range(2):
            packed[level, c] = jnp.concatenate([mixes[level, c, 0], mixes[level, c, 1]], axis=1)
        if level == 0:
            weights[0] = packed[0]
        elif level < bits:
            there = early if level == last else weights.at[level]
            for c in range(2):
                copy, target, index = straight(level, c)

                @pl.when(target != me)
                def _():
                    copy.start()

                @pl.when(target == me)
                def _():
                    there[index] = packed[level, c]
        else:

            @pl.when(home != me)
            def _():
                direct.start()

            @pl.when(home == me)
            def _():
                weights[bits] = packed[bits]

            @pl.when(apart)
            def _():
                around.start()

            @pl.when(jnp.logical_not(apart) & (home != me))
            def _():
                beside.start()

    def forward_last():
        for index in range(2):

            @pl.when(comes(ahead, index) != me)
            def _():
                remote(
                    packed.at[last, 0], early.at[index],
                    w_send.at[last, 0], w_recv.at[last, index], me,
                ).wait_recv()

        weights[last, mine[last]] = early[mine[last]]
        hop.start()

    def forward_relay():
        @pl.when(jnp.logical_not(apart))
        def _():
            around.wait_recv()
            onward.start()

    def take_weights(level):
        if level == 0:
            pass
        elif level < last:
            for index in range(2):

                @pl.when(comes(places[level], index) != me)
                def _():
                    remote(
                        packed.at[level, 0], weights.at[level, index],
                        w_send.at[level, 0], w_recv.at[level, index], me,
                    ).wait_recv()
        elif level == last:
            hop.wait_recv()
        else:

            @pl.when(home != me)
            def _():
                direct.wait_recv()
                beside.wait_recv()

        for index in range(2):
            w_hi[level, index], w_lo[level, index] = split(weights[level, index])

    def mixed(level, index, one, other):
        pair = [jnp.concatenate([a, b], axis=0) for a, b in zip(one, other)]
        return product((w_hi[level, index], w_lo[level, index]), pair)

    def task(s, c):
        if s == 0:

            @pl.when(c == 0)
            def _():
                load_p.wait()
                for n in range(2):
                    p_hi[n], p_lo[n] = split(pbuf[n])

            load_x(c).wait()
            for n in range(2):
                values[0][c, n] = product((p_hi[n], p_lo[n]), split(xbuf[c % 2, n]))
            pl.when(c + 2 < chunks)(lambda: load_x(c + 2).start())
        else:
            slot, full, level = steps[s - 1]
            bit = mine[slot]
            columns = pl.ds(pl.multiple_of(c * width, width), width)
            out = o_ref.at[:, :, columns] if s == count else values[s].at[c]
            if level is not None:
                pl.when(c == 0)(lambda: take_weights(level))
            transfer(s - 1, c).wait_recv()
            own, other = values[s - 1].at[c], arrived[s - 1].at[c]
            if full:
                for n in range(2):
                    out[n] = mixed(level, n, split(own[n]), split(other[n]))
            elif level is None:
                out[bit] = own[bit]
                out[1 - bit] = other[...]
            else:
                a, b = split(own[bit]), split(other[...])
                out[bit] = mixed(level, bit, a, b)
                out[1 - bit] = mixed(level, 1 - bit, b, a)
        if s < count:
            transfer(s, c).start()

    timetable = order(bits, count, chunks)

    def due(t, *kinds):
        words = [0] * (len(timetable) // 31 + 1)
        for i, tasks in enumerate(timetable):
            words[i // 31] |= any(kind in tasks for kind in kinds) << (i % 31)
        word = jnp.int32(words[0])
        for i, other in enumerate(words[1:]):
            word = jnp.where(t >= 31 * (i + 1), other, word)
        return lax.shift_right_logical(word, t % 31) % 2

    def tick(t, carry):
        done = list(carry)
        for s in reversed(range(count + 1)):
            now = due(t, s)
            pl.when(now == 1)(functools.partial(task, s, done[s]))
            done[s] = done[s] + now
        others = [(100 + level, functools.partial(send_weights, level)) for level in range(levels)]
        others += [(200, forward_last), (201, forward_relay)]

        @pl.when(due(t, *(kind for kind, _ in others)) == 1)
        def _():
            for kind, action in others:
                pl.when(due(t, kind) == 1)(action)

        return tuple(done)

    pl.semaphore_wait(barrier, greeted)
    lax.fori_loop(0, len(timetable), tick, (jnp.int32(0),) * (count + 1))

    def drain(c, carry):
        for s in range(count):
            transfer(s, c).wait_send()
        return carry

    lax.fori_loop(0, chunks, drain, 0)
    for level in range(1, bits):
        for c in range(2):
            copy, target, _ = straight(level, c)
            pl.when(target != me)(copy.wait_send)
    hop.wait_send()
    pl.when(home != me)(direct.wait_send)
    pl.when(apart)(around.wait_send)
    pl.when(jnp.logical_not(apart) & (home != me))(beside.wait_send)
    pl.when(jnp.logical_not(apart))(onward.wait_send)


def butterfly(sizes, data, proj, mix):
    _, leaf, rhs = data.shape
    k = proj.shape[1]
    levels = mix.shape[0]
    bits = levels - 1
    width = rhs // CHUNKS
    steps, _, _ = plan(bits)
    f32, bf16 = jnp.float32, jnp.bfloat16
    held = [pltpu.VMEM((CHUNKS, 2, k, width), f32) for _ in steps]
    landed = [pltpu.VMEM((CHUNKS,) + ((2,) if full else ()) + (k, width), f32) for _, full, _ in steps]
    dma = pltpu.SemaphoreType.DMA
    return pl.pallas_call(
        functools.partial(butterfly_kernel, sizes),
        out_shape=jax.ShapeDtypeStruct((2, k, rhs), f32),
        in_specs=[pl.BlockSpec(memory_space=pltpu.HBM)] * 3,
        out_specs=pl.BlockSpec(memory_space=pltpu.VMEM),
        scratch_shapes=held + landed + [
            pltpu.VMEM((2, 2, leaf, width), f32),
            pltpu.VMEM((2, k, leaf), f32),
            pltpu.VMEM((2, k, leaf), bf16),
            pltpu.VMEM((2, k, leaf), bf16),
            pltpu.VMEM((levels, 2, 2, k, k), f32),
            pltpu.VMEM((levels, 2, k, 2 * k), f32),
            pltpu.VMEM((levels, 2, k, 2 * k), f32),
            pltpu.VMEM((2, k, 2 * k), f32),
            pltpu.VMEM((2, k // 2, 2 * k), f32),
            pltpu.VMEM((levels, 2, k, 2 * k), bf16),
            pltpu.VMEM((levels, 2, k, 2 * k), bf16),
            dma((2,)),
            dma,
            dma((levels,)),
            dma((len(steps), CHUNKS)),
            dma((len(steps), CHUNKS)),
            dma((levels + 1, 2)),
            dma((levels + 1, 2)),
        ],
        compiler_params=pltpu.CompilerParams(
            collective_id=0, has_side_effects=True, vmem_limit_bytes=(46 + levels) * 2**20
        ),
    )(data, proj, mix)


def shards(right_sides, projector, mixing, expander):
    sizes = tuple(lax.axis_size(name) for name in AXES)
    proj = jnp.swapaxes(projector[:, 0], 1, 2)
    return expand(jnp.swapaxes(expander, 1, 2), butterfly(sizes, right_sides[:, 0], proj, mixing[:, :, 0]))


def solution(mesh):
    placed = (
        P(None, AXES, None, None),
        P(None, AXES, None, None),
        P(None, None, AXES, None, None, None),
        P(AXES, None, None),
    )
    return jax.shard_map(
        shards, mesh=mesh, in_specs=placed, out_specs=P(AXES, None, None), check_vma=False
    )
```

```python
import functools

import jax
import jax.numpy as jnp
from jax import lax
from jax.experimental import pallas as pl
from jax.experimental.pallas import tpu as pltpu
from jax.sharding import PartitionSpec as P

AXES = ("gx", "gy", "gz")
CHUNKS = 8
ORDER = (
    15, 13, 0, 0, 12, 21, 0, 14, 11, 10, 1, 0, 1, 2, 2, 1, 3, 2, 0, 0, 3, 20, 4, 3, 1, 2, 1, 5, 0, 4, 2, 1, 3, 5, 6, 4,
    2, 5, 4, 3, 1, 0, 6, 3, 6, 4, 5, 2, 1, 5, 4, 7, 7, 6, 2, 3, 5, 7, 6, 4, 3, 6, 5, 7, 4, 6, 5, 7, 8, 6, 8, 7,
    8, 7, 8, 8, 7, 8, 8, 8,
)


def split(x):
    hi = x.astype(jnp.bfloat16)
    lo = (x - hi.astype(jnp.float32)).astype(jnp.bfloat16)
    return hi, lo


def product(a, b, over=((1,), (0,))):
    def dot(x, y):
        return lax.dot_general(x, y, (over, ((), ())), preferred_element_type=jnp.float32)

    return dot(a[0], b[0]) + (dot(a[0], b[1]) + dot(a[1], b[0]))


def expand_kernel(e_ref, c_ref, o_ref):
    o_ref[0] = product(split(e_ref[0]), split(c_ref[0]), ((0,), (0,)))


def expand(expander, coeffs):
    nodes, k, leaf = expander.shape
    rhs = coeffs.shape[2]
    return pl.pallas_call(
        expand_kernel,
        grid=(nodes,),
        in_specs=[
            pl.BlockSpec((1, k, leaf), lambda n: (n, 0, 0)),
            pl.BlockSpec((1, k, rhs), lambda n: (n, 0, 0)),
        ],
        out_specs=pl.BlockSpec((1, leaf, rhs), lambda n: (n, 0, 0)),
        out_shape=jax.ShapeDtypeStruct((nodes, leaf, rhs), jnp.float32),
        compiler_params=pltpu.CompilerParams(vmem_limit_bytes=32 * 2**20),
    )(expander, coeffs)


def plan(bits):
    slots, local = list(range(bits)), bits
    steps, places = [], {}

    def swap(slot, level):
        nonlocal local
        slots[slot], local = local, slots[slot]
        steps.append((slot, False, level))
        if level is not None:
            places[level] = (tuple(slots), local)

    def show(slot):
        steps.append((slot, True, slot))
        places[slot] = (tuple(slots), local)

    half = bits // 2
    show(0)
    for k in range(1, half):
        swap(k, k)
    if bits % 2:
        show(half)
    for k in reversed(range(1, half)):
        swap(bits - 1 - k, bits - 1 - k)
        swap(k, None)
    swap(0, None)
    ahead = (tuple(slots), local)
    swap(bits - 1, bits - 1)
    swap(0, bits)
    return steps, places, ahead


def order(bits, count, chunks):
    tasks = list(ORDER)
    whole = [tasks.count(s) == chunks for s in range(count + 1)] + [tasks.count(10 + i) for i in range(bits + 1)]
    if not all(whole) or len(tasks) != (count + 1) * chunks + bits + 3:
        timed = [(3 * c + 4 * s, s) for c in range(chunks) for s in range(count + 1)]
        timed += [(l - bits, 100 + l) for l in range(bits + 1)] + [(0, 200), (0, 201)]
        tasks = [task for _, task in sorted(timed)]
    else:
        tasks = [task if task < 10 else 90 + task if task < 20 else 180 + task for task in tasks]
    ticks, at = [[]], -count - 1
    for task in tasks:
        rank = task if task >= 100 else -task
        if rank <= at:
            ticks.append([])
        ticks[-1].append(task)
        at = rank
    return ticks


def butterfly_kernel(sizes, x_hbm, p_hbm, mix_hbm, o_ref, *scratch):
    bits = sum(size.bit_length() - 1 for size in sizes)
    levels = bits + 1
    steps, places, ahead = plan(bits)
    count = len(steps)
    values, arrived = scratch[:count], scratch[count : 2 * count]
    (
        xbuf, pbuf, p_hi, p_lo, mixes, packed, weights, early, relay, w_hi, w_lo,
        x_sem, p_sem, mix_sem, send, recv, w_send, w_recv,
    ) = scratch[2 * count :]
    chunks, _, k, width = values[0].shape
    part = k // 2
    coords = [lax.axis_index(name) for name in AXES]
    me = (coords[0] * sizes[1] + coords[1]) * sizes[2] + coords[2]

    def bit_of(device, b):
        return (device // (1 << b)) % 2

    def flip(device, b):
        return device + (1 - 2 * bit_of(device, b)) * (1 << b)

    def place(d):
        return {
            "gx": d // (sizes[1] * sizes[2]),
            "gy": (d // sizes[2]) % sizes[1],
            "gz": d % sizes[2],
        }

    mine = [bit_of(me, b) for b in range(bits)]

    def goes(layout, c):
        slots, local = layout
        of_node = mine + [c]
        return sum(of_node[slot] * (1 << b) for b, slot in enumerate(slots)), of_node[local]

    def comes(layout, index):
        slots, local = layout
        of_node = [None] * (bits + 1)
        for b, slot in enumerate(slots):
            of_node[slot] = mine[b]
        of_node[local] = index
        return sum(of_node[b] * (1 << b) for b in range(bits))

    def reverse(device):
        return sum(bit_of(device, b) * (1 << (bits - 1 - b)) for b in range(bits))

    def remote(src, dst, s_sem, r_sem, target):
        return pltpu.make_async_remote_copy(
            src_ref=src,
            dst_ref=dst,
            send_sem=s_sem,
            recv_sem=r_sem,
            device_id=place(target),
            device_id_type=pl.DeviceIdType.MESH,
        )

    def transfer(s, c):
        slot, full, _ = steps[s]
        src = values[s].at[c] if full else values[s].at[c, 1 - mine[slot]]
        return remote(src, arrived[s].at[c], send.at[s, c], recv.at[s, c], flip(me, slot))

    def straight(level, c):
        target, index = goes(ahead if level == bits - 1 else places[level], c)
        there = early if level == bits - 1 else weights.at[level]
        copy = remote(
            packed.at[level, c], there.at[index],
            w_send.at[level, c], w_recv.at[level, index], target,
        )
        return copy, target, index

    last = bits - 1
    hop = remote(
        early.at[1 - mine[last]], weights.at[last, mine[last]],
        w_send.at[bits + 1, 0], w_recv.at[bits + 1, 0], flip(me, last),
    )
    home = reverse(me)
    apart = mine[0] != mine[last]
    lower, upper = pl.ds(0, part), pl.ds(part, part)
    direct = remote(
        packed.at[bits, :, lower], weights.at[bits, :, lower],
        w_send.at[bits, 0], w_recv.at[bits, 0], home,
    )
    beside = remote(
        packed.at[bits, :, upper], weights.at[bits, :, upper],
        w_send.at[bits, 1], w_recv.at[bits, 1], home,
    )
    around = remote(
        packed.at[bits, :, upper], relay, w_send.at[bits, 1], w_recv.at[bits + 1, 1], flip(me, 0)
    )
    onward = remote(
        relay, weights.at[bits, :, upper],
        w_send.at[bits + 1, 1], w_recv.at[bits, 1], reverse(flip(me, 0)),
    )

    def when(condition, action):
        pl.when(condition)(action)

    def greet(target):
        pl.semaphore_signal(
            barrier, inc=1, device_id=place(target), device_id_type=pl.DeviceIdType.MESH
        )

    barrier = pltpu.get_barrier_semaphore()
    greeted = jnp.int32(bits)
    for b in range(bits):
        greet(flip(me, b))
    layouts = [places[level] for level in range(1, last)] + [ahead]
    for layout in layouts:
        for c in range(2):
            source = comes(layout, c)
            when(source != me, functools.partial(greet, source))
            greeted = greeted + (goes(layout, c)[0] != me).astype(jnp.int32)
    when(home != me, functools.partial(greet, home))
    greeted = greeted + (home != me).astype(jnp.int32)
    when(apart, functools.partial(greet, flip(home, 0)))
    greeted = greeted + jnp.logical_not(apart).astype(jnp.int32)

    def load_x(c):
        return pltpu.make_async_copy(
            x_hbm.at[:, :, pl.ds(pl.multiple_of(c * width, width), width)],
            xbuf.at[c % 2], x_sem.at[c % 2],
        )

    load_p = pltpu.make_async_copy(p_hbm, pbuf, p_sem)

    def load_mix(level):
        return pltpu.make_async_copy(mix_hbm.at[level], mixes.at[level], mix_sem.at[level])

    load_mix(bits).start()
    load_p.start()
    load_x(0).start()
    for level in range(bits):
        load_mix(level).start()
    load_x(1).start()

    def send_weights(level):
        load_mix(level).wait()
        for c in range(2):
            packed[level, c] = jnp.concatenate([mixes[level, c, 0], mixes[level, c, 1]], axis=1)
        if level == 0:
            weights[0] = packed[0]
        elif level < bits:
            there = early if level == last else weights.at[level]
            for c in range(2):
                copy, target, index = straight(level, c)

                @pl.when(target != me)
                def _():
                    copy.start()

                @pl.when(target == me)
                def _():
                    there[index] = packed[level, c]
        else:

            @pl.when(home != me)
            def _():
                direct.start()

            @pl.when(home == me)
            def _():
                weights[bits] = packed[bits]

            @pl.when(apart)
            def _():
                around.start()

            @pl.when(jnp.logical_not(apart) & (home != me))
            def _():
                beside.start()

    def forward_last():
        for index in range(2):

            @pl.when(comes(ahead, index) != me)
            def _():
                remote(
                    packed.at[last, 0], early.at[index],
                    w_send.at[last, 0], w_recv.at[last, index], me,
                ).wait_recv()

        weights[last, mine[last]] = early[mine[last]]
        hop.start()

    def forward_relay():
        @pl.when(jnp.logical_not(apart))
        def _():
            around.wait_recv()
            onward.start()

    def take_weights(level):
        if level == 0:
            pass
        elif level < last:
            for index in range(2):

                @pl.when(comes(places[level], index) != me)
                def _():
                    remote(
                        packed.at[level, 0], weights.at[level, index],
                        w_send.at[level, 0], w_recv.at[level, index], me,
                    ).wait_recv()
        elif level == last:
            hop.wait_recv()
        else:

            @pl.when(home != me)
            def _():
                direct.wait_recv()
                beside.wait_recv()

        for index in range(2):
            w_hi[level, index], w_lo[level, index] = split(weights[level, index])

    def mixed(level, index, one, other):
        pair = [jnp.concatenate([a, b], axis=0) for a, b in zip(one, other)]
        high = w_hi[level, index]
        weight = jnp.concatenate([high, high, w_lo[level, index]], axis=1)
        stacked = jnp.concatenate([pair[0], pair[1], pair[0]], axis=0)
        return jnp.dot(weight, stacked, preferred_element_type=jnp.float32)

    def task(s, c):
        if s == 0:

            @pl.when(c == 0)
            def _():
                load_p.wait()
                for n in range(2):
                    p_hi[n], p_lo[n] = split(pbuf[n])

            load_x(c).wait()
            for n in range(2):
                values[0][c, n] = product((p_hi[n], p_lo[n]), split(xbuf[c % 2, n]))
            pl.when(c + 2 < chunks)(lambda: load_x(c + 2).start())
        else:
            slot, full, level = steps[s - 1]
            bit = mine[slot]
            columns = pl.ds(pl.multiple_of(c * width, width), width)
            out = o_ref.at[:, :, columns] if s == count else values[s].at[c]
            if level is not None:
                pl.when(c == 0)(lambda: take_weights(level))
            transfer(s - 1, c).wait_recv()
            own, other = values[s - 1].at[c], arrived[s - 1].at[c]
            if full:
                for n in range(2):
                    out[n] = mixed(level, n, split(own[n]), split(other[n]))
            elif level is None:
                out[bit] = own[bit]
                out[1 - bit] = other[...]
            else:
                a, b = split(own[bit]), split(other[...])
                out[bit] = mixed(level, bit, a, b)
                out[1 - bit] = mixed(level, 1 - bit, b, a)
        if s < count:
            transfer(s, c).start()

    timetable = order(bits, count, chunks)

    def due(t, *kinds):
        words = [0] * (len(timetable) // 31 + 1)
        for i, tasks in enumerate(timetable):
            words[i // 31] |= any(kind in tasks for kind in kinds) << (i % 31)
        word = jnp.int32(words[0])
        for i, other in enumerate(words[1:]):
            word = jnp.where(t >= 31 * (i + 1), other, word)
        return lax.shift_right_logical(word, t % 31) % 2

    def tick(t, carry):
        done = list(carry)
        for s in reversed(range(count + 1)):
            now = due(t, s)
            pl.when(now == 1)(functools.partial(task, s, done[s]))
            done[s] = done[s] + now
        others = [(100 + level, functools.partial(send_weights, level)) for level in range(levels)]
        others += [(200, forward_last), (201, forward_relay)]

        @pl.when(due(t, *(kind for kind, _ in others)) == 1)
        def _():
            for kind, action in others:
                pl.when(due(t, kind) == 1)(action)

        return tuple(done)

    pl.semaphore_wait(barrier, greeted)
    lax.fori_loop(0, len(timetable), tick, (jnp.int32(0),) * (count + 1))

    def drain(c, carry):
        for s in range(count):
            transfer(s, c).wait_send()
        return carry

    lax.fori_loop(0, chunks, drain, 0)
    for level in range(1, bits):
        for c in range(2):
            copy, target, _ = straight(level, c)
            pl.when(target != me)(copy.wait_send)
    hop.wait_send()
    pl.when(home != me)(direct.wait_send)
    pl.when(apart)(around.wait_send)
    pl.when(jnp.logical_not(apart) & (home != me))(beside.wait_send)
    pl.when(jnp.logical_not(apart))(onward.wait_send)


def butterfly(sizes, data, proj, mix):
    _, leaf, rhs = data.shape
    k = proj.shape[1]
    levels = mix.shape[0]
    bits = levels - 1
    width = rhs // CHUNKS
    steps, _, _ = plan(bits)
    f32, bf16 = jnp.float32, jnp.bfloat16
    held = [pltpu.VMEM((CHUNKS, 2, k, width), f32) for _ in steps]
    landed = [pltpu.VMEM((CHUNKS,) + ((2,) if full else ()) + (k, width), f32) for _, full, _ in steps]
    dma = pltpu.SemaphoreType.DMA
    return pl.pallas_call(
        functools.partial(butterfly_kernel, sizes),
        out_shape=jax.ShapeDtypeStruct((2, k, rhs), f32),
        in_specs=[pl.BlockSpec(memory_space=pltpu.HBM)] * 3,
        out_specs=pl.BlockSpec(memory_space=pltpu.VMEM),
        scratch_shapes=held + landed + [
            pltpu.VMEM((2, 2, leaf, width), f32),
            pltpu.VMEM((2, k, leaf), f32),
            pltpu.VMEM((2, k, leaf), bf16),
            pltpu.VMEM((2, k, leaf), bf16),
            pltpu.VMEM((levels, 2, 2, k, k), f32),
            pltpu.VMEM((levels, 2, k, 2 * k), f32),
            pltpu.VMEM((levels, 2, k, 2 * k), f32),
            pltpu.VMEM((2, k, 2 * k), f32),
            pltpu.VMEM((2, k // 2, 2 * k), f32),
            pltpu.VMEM((levels, 2, k, 2 * k), bf16),
            pltpu.VMEM((levels, 2, k, 2 * k), bf16),
            dma((2,)),
            dma,
            dma((levels,)),
            dma((len(steps), CHUNKS)),
            dma((len(steps), CHUNKS)),
            dma((levels + 1, 2)),
            dma((levels + 1, 2)),
        ],
        compiler_params=pltpu.CompilerParams(
            collective_id=0, has_side_effects=True, vmem_limit_bytes=(46 + levels) * 2**20
        ),
    )(data, proj, mix)


def shards(right_sides, projector, mixing, expander):
    sizes = tuple(lax.axis_size(name) for name in AXES)
    proj = jnp.swapaxes(projector[:, 0], 1, 2)
    return expand(jnp.swapaxes(expander, 1, 2), butterfly(sizes, right_sides[:, 0], proj, mixing[:, :, 0]))


def solution(mesh):
    placed = (
        P(None, AXES, None, None),
        P(None, AXES, None, None),
        P(None, None, AXES, None, None, None),
        P(AXES, None, None),
    )
    return jax.shard_map(
        shards, mesh=mesh, in_specs=placed, out_specs=P(AXES, None, None), check_vma=False
    )
```
